128 devices in a mesh: layer: 8 (over x, core), rows: 16 (over z, y).
Axes of the slice: x: 4, y: 4, z: 4, core: 2. Of those that a mesh axis runs over, the one named last changes fastest.
Arguments:
- key_weight: bfloat16 [8, 8192, 512], P('layer', 'rows'), may hold values from -0.0625 to 0.0625
- value_weight: bfloat16 [8, 8192, 512], P('layer', 'rows'), may hold values from -0.0625 to 0.0625
- key_grad: bfloat16 [8, 8192, 512], P('layer', 'rows'), may hold values from -8000 to 8000
- value_grad: bfloat16 [8, 8192, 512], P('layer', 'rows'), may hold values from -8000 to 8000
Outputs:
- key_update: bfloat16 [8, 8192, 512], P('layer', 'rows')
- value_update: bfloat16 [8, 8192, 512], P('layer', 'rows')
- key_dual: float32 [8, 512, 512], P('layer', 'rows')
- value_dual: float32 [8, 512, 512], P('layer', 'rows')
The draws below stay inside these ranges and needn't reach their ends.
All inputs are finite; a program needn't handle non-finite values.
Results may differ from the reference program's by a relative error of at most 0.033.
Values may be sent and summed in bfloat16 or wider, within the bound.
No kernel may reach another device: no remote copies, remote signals or barrier semaphores. Data moves between devices by JAX's collectives and lax.ppermute only.
A program may use at most 64 MiB of HBM per device.

```python
import jax
import jax.numpy as jnp
from jax import lax

D = 8192
COLS = 512
DUAL_ITERS = 2
NS_STEPS = 3
LAYERS = 8


def sign_terms(key, strengths):
    result = jnp.zeros((LAYERS, D, COLS), jnp.float32)
    for number, strength in enumerate(strengths):
        row_key, column_key = jax.random.split(jax.random.fold_in(key, number))
        row_sign = jax.random.rademacher(row_key, (LAYERS, D, 1), jnp.float32)
        column_sign = jax.random.rademacher(column_key, (LAYERS, 1, COLS), jnp.float32)
        result = result + strength * row_sign * column_sign
    return result


def grad_draw(key, salt):
    base_key = jax.random.fold_in(key, salt)
    noise_key = jax.random.fold_in(base_key, 0)
    row_key = jax.random.fold_in(base_key, 1)
    column_key = jax.random.fold_in(base_key, 2)
    outer_key = jax.random.fold_in(base_key, 4)
    layer_pos = jnp.arange(LAYERS, dtype=jnp.float32) / max(LAYERS - 1, 1)
    row_pos = jnp.arange(D, dtype=jnp.float32) / (D - 1)
    row_scale = jnp.exp(jax.random.uniform(row_key, (D,), jnp.float32, 0.0, jnp.log(10.0))) * jnp.power(3.0, 0.5 * row_pos)
    column_scale = jnp.exp(jax.random.uniform(column_key, (COLS,), jnp.float32, 0.0, jnp.log(10.0)))
    layer_scale = jnp.power(6.0, layer_pos)
    noise = jnp.clip(jax.random.normal(noise_key, (LAYERS, D, COLS), jnp.float32), -3.0, 3.0)
    noise = noise + sign_terms(outer_key, [2.0, 1.5])
    values = noise * layer_scale[:, None, None] * row_scale[None, :, None] * column_scale[None, None, :]
    return values.astype(jnp.bfloat16)


def draw_key_grad(key, part):
    return grad_draw(key, 11)


def draw_value_grad(key, part):
    return grad_draw(key, 23)


def levels(own_key, shape, cuts, low, top_value):
    loudness = 1.0
    for dim, parts in cuts:
        steps = jax.random.uniform(jax.random.fold_in(jax.random.fold_in(own_key, 6), dim), (parts,), jnp.float32, low / len(cuts), top_value / len(cuts))
        loudness = loudness * jnp.repeat(jnp.exp(steps), shape[dim] // parts).reshape((-1,) + (1,) * (len(shape) - 1 - dim))
    return loudness


def gaussian(own_key, dims, spread, most, pieces=(), kind=jnp.bfloat16):
    values = jax.random.normal(own_key, dims, jnp.float32) * spread
    if len(pieces) > 0:
        values = levels(own_key, dims, pieces, -0.22, 0.18) * values
    return jnp.clip(values, min=-most, max=most).astype(kind)


def setup_inputs(seed: int = 0) -> dict:
    splits = jax.random.split(jax.random.key(seed), 5)
    key_weight = gaussian(splits[0], (LAYERS, D, COLS), D ** -0.5, 0.0625, ((0, 8), (1, 16)))
    value_weight = gaussian(splits[1], (LAYERS, D, COLS), D ** -0.5, 0.0625, ((0, 8), (1, 16)))
    key_grad = draw_key_grad(jax.random.fold_in(splits[4], 71), 0)
    value_grad = draw_value_grad(jax.random.fold_in(splits[4], 71), 0)
    return {"key_weight": key_weight, "value_weight": value_weight, "key_grad": key_grad, "value_grad": value_grad}


first_coeff = 3.4445
third_coeff = -4.775
fifth_coeff = 2.0315
learn_rate = 0.1
dual_rate = 4.0
clip_target = 0.02
epsilon = 1e-06
highest = lax.Precision.HIGHEST

def gram_of(matrix):
    return jnp.dot(matrix.T, matrix, preferred_element_type=jnp.float32)

def make_poly(gram):
    quartic = jnp.dot(gram, gram, precision=highest)
    return (third_coeff * gram + fifth_coeff * quartic).astype(jnp.bfloat16)

def orthogonalize(shifted):
    squares = jnp.sum(jnp.square(shifted.astype(jnp.float32)))
    poly = make_poly(gram_of(shifted) / (squares + epsilon))
    iterate = ((first_coeff * shifted.astype(jnp.float32) + jnp.dot(shifted, poly, preferred_element_type=jnp.float32)) / jnp.sqrt(squares + epsilon)).astype(jnp.bfloat16)
    for repeat in range(NS_STEPS - 1):
        poly = make_poly(gram_of(iterate))
        iterate = (first_coeff * iterate.astype(jnp.float32) + jnp.dot(iterate, poly, preferred_element_type=jnp.float32)).astype(jnp.bfloat16)
    return iterate

def one_matrix(weight, grad, clip):
    dual = jnp.zeros((weight.shape[1], weight.shape[1]), jnp.float32)
    iterate = weight
    for iteration in range(DUAL_ITERS):
        shift = (4.0 * dual).astype(jnp.bfloat16)
        shifted = (clip * grad.astype(jnp.float32) + jnp.dot(weight, shift, preferred_element_type=jnp.float32)).astype(jnp.bfloat16)
        iterate = orthogonalize(shifted)
        cross = jnp.dot(weight.T, iterate, preferred_element_type=jnp.float32)
        dual = dual + dual_rate * -learn_rate * (cross + cross.T)
    update = (-learn_rate * iterate.astype(jnp.float32)).astype(jnp.bfloat16)
    return (update, dual)

def reference(key_weight, value_weight, key_grad, value_grad):
    total = jnp.sum(jnp.square(key_grad.astype(jnp.float32))) + jnp.sum(jnp.square(value_grad.astype(jnp.float32)))
    entries = 2.0 * LAYERS * D * COLS
    clip = clip_target / jnp.sqrt(total / entries + epsilon)

    def per_layer(pair):
        return one_matrix(pair[0], pair[1], clip)
    key_update, key_dual = lax.map(per_layer, (key_weight, key_grad))
    value_update, value_dual = lax.map(per_layer, (value_weight, value_grad))
    return (key_update, value_update, key_dual, value_dual)
```

```python
import functools

import jax
import jax.numpy as jnp
from jax import lax
from jax.experimental import pallas as pl
from jax.experimental.pallas import tpu as pltpu
from jax.sharding import Mesh
from jax.sharding import PartitionSpec as P


A1, A3, A5 = 3.4445, -4.775, 2.0315
LR = 0.1
STEP = -0.4
CLIP = 0.02
EPS = 1e-06
F32, BF16 = jnp.float32, jnp.bfloat16
T = 128
VMEM = pl.BlockSpec(memory_space=pltpu.VMEM)
SMEM = pl.BlockSpec(memory_space=pltpu.SMEM)


def params():
    return pltpu.CompilerParams(vmem_limit_bytes=56 * 1024 * 1024)


def dot(a, b):
    return jnp.dot(a, b, preferred_element_type=F32)


def dot_tl(a, b):
    return lax.dot_general(a, b, (((0,), (0,)), ((), ())), preferred_element_type=F32)


def dot_tr(a, b):
    return lax.dot_general(a, b, (((1,), (1,)), ((), ())), preferred_element_type=F32)


def upper(n):
    return [(i, j) for i in range(n) for j in range(i, n)]


def put_block(scr, per, b, value):
    scr[b // per, pl.ds((b % per) * T, T), :] = value


def get_block(scr, per, b, base=0):
    return scr[b // per, pl.ds(base + (b % per) * T, T), :]


def gram_g_kernel(nb, me_ref, gk, gv, own, s1, s2, s3, ss, scr):
    per = nb * (nb + 1) // 2 * 2 // 4
    b = 0
    total = jnp.zeros(ss.shape, F32)
    for g in (gk, gv):
        for i in range(nb):
            row = dot_tl(g[:, i * T : (i + 1) * T], g[:, i * T :])
            for j in range(i, nb):
                put_block(scr, per, b, row[:, (j - i) * T : (j - i + 1) * T])
                b += 1
        for i in range(nb):
            part = g[:, i * T : (i + 1) * T].astype(F32)
            total = total + jnp.sum((part * part).reshape(-1, 8, T), axis=0)
    ss[...] = total
    me = me_ref[0]
    own[...] = scr[me]
    for s, out in ((1, s1), (2, s2), (3, s3)):
        out[...] = scr[lax.rem(me + s, 4)].astype(BF16)


def gram_w_kernel(nb, me_ref, wk, wv, gk, gv, own, s1, s2, s3, scr):
    per = (2 * nb * nb + nb * (nb + 1)) // 4
    b = 0
    for w, g in ((wk, gk), (wv, gv)):
        for i in range(nb):
            row = dot_tl(w[:, i * T : (i + 1) * T], g[...])
            for j in range(nb):
                put_block(scr, per, b, row[:, j * T : (j + 1) * T].astype(BF16))
                b += 1
    for w in (wk, wv):
        for i in range(nb):
            row = dot_tl(w[:, i * T : (i + 1) * T], w[:, i * T :])
            for j in range(i, nb):
                put_block(scr, per, b, row[:, (j - i) * T : (j - i + 1) * T].astype(BF16))
                b += 1
    me = me_ref[0]
    own[...] = scr[me]
    for s, out in ((1, s1), (2, s2), (3, s3)):
        out[...] = scr[lax.rem(me + s, 4)]


def split_hi_lo(out, n, total, squares):
    hi = total.astype(BF16)
    out[0:n] = hi
    out[n : 2 * n] = (total - hi.astype(F32)).astype(BF16)
    hi = squares.astype(BF16)
    out[2 * n : 2 * n + 16] = jnp.concatenate([hi.astype(F32), squares - hi.astype(F32)], 0).astype(BF16)


def sum_g1_kernel(own, r1, r2, r3, ss, out):
    n = own.shape[0]
    total = own[...] + r1[...].astype(F32) + r2[...].astype(F32) + r3[...].astype(F32)
    split_hi_lo(out, n, total, ss[...])


def sum_g2_kernel(m0, m1, m2, m3, out):
    n = (m0.shape[0] - 16) // 2
    total, squares = 0.0, 0.0
    for m in (m0, m1, m2, m3):
        total = total + (m[0:n].astype(F32) + m[n : 2 * n].astype(F32))
        tail = m[2 * n : 2 * n + 16].astype(F32)
        squares = squares + (tail[0:8] + tail[8:16])
    split_hi_lo(out, n, total, squares)


def sum_w_kernel(m0, m1, m2, m3, out):
    out[...] = (m0[...].astype(F32) + m1[...].astype(F32) + m2[...].astype(F32) + m3[...].astype(F32)).astype(BF16)


def collect(me, scr, parts):
    for s, part in enumerate(parts):
        scr[lax.rem(me + 4 - s, 4)] = part[...]


def newton_schulz(m, mb, p_refs):
    for k, p_ref in enumerate(p_refs):
        mb[...] = m[...].astype(BF16)
        p_ref[...] = (A3 * m[...] + A5 * dot(mb[...], mb[...])).astype(BF16)
        if k < 2:
            m[...] = A1 * m[...] + dot(mb[...], p_ref[...])
            mb[...] = m[...].astype(BF16)
            m[...] = A1 * m[...] + dot(mb[...], p_ref[...])


def first_kernel(nb, entries, me_ref, m0, m1, m2, m3, gg, ps, scal, scr, m, mb):
    tri = nb * (nb + 1) // 2
    per = tri * 2 // 4
    n = per * T
    me = me_ref[0]
    collect(me, scr, (m0, m1, m2, m3))
    squares = jnp.zeros((8, T), F32)
    for part in (m0, m1, m2, m3):
        tail = part[2 * n : 2 * n + 16].astype(F32)
        squares = squares + (tail[0:8] + tail[8:16])
    total = jnp.sum(squares)
    clip = CLIP / jnp.sqrt(total / entries + EPS)
    rows = lax.broadcasted_iota(jnp.int32, (T, T), 0)
    cols = lax.broadcasted_iota(jnp.int32, (T, T), 1)
    scal[...] = jnp.full(scal.shape, clip, F32)
    for which in range(2):
        trace = 0.0
        for pos, (i, j) in enumerate(upper(nb)):
            b = which * tri + pos
            block = get_block(scr, per, b).astype(F32) + get_block(scr, per, b, n).astype(F32)
            block = block * (clip * clip)
            gg[which, i * T : (i + 1) * T, j * T : (j + 1) * T] = block
            if i == j:
                trace = trace + jnp.sum(jnp.where(rows == cols, block, 0.0))
            else:
                gg[which, j * T : (j + 1) * T, i * T : (i + 1) * T] = block.T
        inverse = 1.0 / (trace + EPS)
        scal[which + 1] = jnp.full(scal.shape[1:], lax.rsqrt(trace + EPS), F32)
        m[...] = gg[which] * inverse
        newton_schulz(m, mb, [ps.at[which, k] for k in range(3)])


def apply_steps(x, p_of, scale):
    for k in range(3):
        x = A1 * x + dot(x.astype(BF16), p_of(k))
        if k == 0:
            x = x * scale
    return x


def second_kernel(
    nb, me_ref, row_ref, m0, m1, m2, m3, gg, ps, scal, wk, wv, gk, gv, uk, uv, dk, dv, scr, wg, ww, s_scr, m, mb, lt, cc, vb, x, p2
):
    tri = nb * (nb + 1) // 2
    per = (2 * nb * nb + 2 * tri) // 4
    depth = dk.shape[0]
    me = me_ref[0]
    collect(me, scr, (m0, m1, m2, m3))
    clip = scal[0, 0:1, 0:1]
    for which, (w, g, u, d) in enumerate(((wk, gk, uk, dk), (wv, gv, uv, dv))):
        for i in range(nb):
            for j in range(nb):
                b = which * nb * nb + i * nb + j
                wg[i * T : (i + 1) * T, j * T : (j + 1) * T] = (clip * get_block(scr, per, b).astype(F32)).astype(BF16)
        for pos, (i, j) in enumerate(upper(nb)):
            b = 2 * nb * nb + which * tri + pos
            block = get_block(scr, per, b)
            ww[i * T : (i + 1) * T, j * T : (j + 1) * T] = block
            if i != j:
                ww[j * T : (j + 1) * T, i * T : (i + 1) * T] = block.astype(F32).T.astype(BF16)
        scale = scal[which + 1, 0:1, 0:1]
        cc[...] = wg[...].astype(F32)
        for k in range(3):
            mb[...] = cc[...].astype(BF16)
            step = A1 * cc[...] + dot(mb[...], ps[which, k])
            cc[...] = step * scale if k == 0 else step
        lt[...] = STEP * (cc[...] + cc[...].T)
        s_scr[...] = (4.0 * lt[...]).astype(BF16)
        cc[...] = wg[...].astype(F32) + dot(ww[...], s_scr[...])
        vb[...] = cc[...].astype(BF16)
        m[...] = gg[which] + dot_tl(wg[...], s_scr[...]) + dot(s_scr[...], vb[...])
        trace = 0.0
        rows = lax.broadcasted_iota(jnp.int32, (T, T), 0)
        cols = lax.broadcasted_iota(jnp.int32, (T, T), 1)
        for i in range(nb):
            block = m[i * T : (i + 1) * T, i * T : (i + 1) * T]
            trace = trace + jnp.sum(jnp.where(rows == cols, block, 0.0))
        m[...] = m[...] * (1.0 / (trace + EPS))
        newton_schulz(m, mb, [p2.at[k] for k in range(3)])
        scale2 = lax.rsqrt(jnp.full((1, 1), trace + EPS, F32))
        x[...] = (clip * g[...].astype(F32) + dot(w[...], s_scr[...])).astype(BF16)
        for k in range(3):
            step = A1 * x[...].astype(F32) + dot(x[...], p2[k])
            if k == 0:
                step = step * scale2
            x[...] = step.astype(BF16)
        u[...] = (-LR * x[...].astype(F32)).astype(BF16)
        start = pl.multiple_of(row_ref[0] * depth, depth)
        here = pl.ds(start, depth)
        left = apply_steps(cc[here, :], lambda k: p2[k], scale2)
        q = A1 * (lax.broadcasted_iota(jnp.int32, (depth, nb * T), 0) + start == lax.broadcasted_iota(jnp.int32, (depth, nb * T), 1)).astype(F32)
        q = q + p2[2, here, :].astype(F32)
        q = A1 * q + dot(q.astype(BF16), p2[1])
        q = (A1 * q + dot(q.astype(BF16), p2[0])) * scale2
        right = dot_tr(q.astype(BF16), vb[...])
        d[...] = lt[here, :] + STEP * (left + right)


def call(kernel, outs, ins, scratch=(), smem=0):
    many = isinstance(outs, list)
    return pl.pallas_call(
        kernel,
        out_shape=[jax.ShapeDtypeStruct(*o) for o in outs] if many else jax.ShapeDtypeStruct(*outs),
        in_specs=[SMEM] * smem + [VMEM] * (len(ins) - smem),
        out_specs=[VMEM] * len(outs) if many else VMEM,
        scratch_shapes=[pltpu.VMEM(*s) for s in scratch],
        compiler_params=params(),
    )(*ins)


CORE_ROWS = ("layer_1", "rows_0", "rows_1")


def shifted_pairs(first, s, nz, ny):
    pairs = []
    for core in range(2):
        for z in range(nz):
            for y in range(ny):
                along_z = (core == 0) == first
                to = (core, (z + s) % nz, y) if along_z else (core, z, (y + s) % ny)
                pairs.append(((core * nz + z) * ny + y, (to[0] * nz + to[1]) * ny + to[2]))
    return pairs


def exchange(values, first):
    return [lax.ppermute(v, CORE_ROWS, shifted_pairs(first, s, 4, 4)) for s, v in zip((1, 2, 3), values)]


def over_layers(ss):
    for pairs in ([(0, 1), (1, 0), (2, 3), (3, 2)], [(0, 3), (3, 0), (1, 2), (2, 1)]):
        ss = ss + lax.ppermute(ss, "layer_0", pairs)
    return ss + lax.ppermute(ss, "layer_1", [(0, 1), (1, 0)])


def on_device(key_weight, value_weight, key_grad, value_grad):
    wk, wv, gk, gv = key_weight[0], value_weight[0], key_grad[0], value_grad[0]
    width = wk.shape[1]
    nb = width // T
    tri = nb * (nb + 1) // 2
    devices = lax.axis_size(("rows_0", "rows_1"))
    entries = 2.0 * wk.size * devices * lax.axis_size(("layer_0", "layer_1"))
    z, y = lax.axis_index("rows_0"), lax.axis_index("rows_1")
    me = jnp.where(lax.axis_index("layer_1") == 0, z, y).astype(jnp.int32).reshape(1)
    row = (z * 4 + y).astype(jnp.int32).reshape(1)
    ng, nw = 2 * tri // 4 * T, (2 * nb * nb + 2 * tri) // 4 * T
    long = 2 * ng + 16

    own_g, *send_g, ss = call(
        functools.partial(gram_g_kernel, nb),
        [((ng, T), F32)] + [((ng, T), BF16)] * 3 + [((8, T), F32)],
        [me, gk, gv],
        [((4, ng, T), F32)],
        1,
    )
    got_g = exchange(send_g, True)
    ss = over_layers(ss)
    own_w, *send_w = call(
        functools.partial(gram_w_kernel, nb),
        [((nw, T), BF16)] * 4,
        [me, wk, wv, gk, gv],
        [((4, nw, T), BF16)],
        1,
    )
    got_w = exchange(send_w, True)
    msg_g = call(sum_g1_kernel, ((long, T), BF16), [own_g, *got_g, ss])
    got_g = exchange([msg_g] * 3, False)
    msg_w = call(sum_w_kernel, ((nw, T), BF16), [own_w, *got_w])
    got_w = exchange([msg_w] * 3, False)
    msg_g = call(sum_g2_kernel, ((long, T), BF16), [msg_g, *got_g])
    got_g = exchange([msg_g] * 3, True)
    msg_w = call(sum_w_kernel, ((nw, T), BF16), [msg_w, *got_w])
    got_w = exchange([msg_w] * 3, True)
    square = (width, width)
    gg, ps, scal = call(
        functools.partial(first_kernel, nb, entries),
        [((2, *square), F32), ((2, 3, *square), BF16), ((3, 8, T), F32)],
        [me, msg_g, *got_g],
        [((4, long, T), BF16), (square, F32), (square, BF16)],
        1,
    )
    depth = width // devices
    uk, uv, dk, dv = call(
        functools.partial(second_kernel, nb),
        [(wk.shape, BF16)] * 2 + [((depth, width), F32)] * 2,
        [me, row, msg_w, *got_w, gg, ps, scal, wk, wv, gk, gv],
        [
            ((4, nw, T), BF16), (square, BF16), (square, BF16), (square, BF16), (square, F32), (square, BF16),
            (square, F32), (square, F32), (square, BF16), (wk.shape, BF16), ((3, *square), BF16),
        ],
        2,
    )
    return (uk[None], uv[None], dk[None], dv[None])


def solution(mesh):
    torus = Mesh(mesh.devices.reshape(4, 2, 4, 4), ("layer_0", "layer_1", "rows_0", "rows_1"))
    placed = P(("layer_0", "layer_1"), ("rows_0", "rows_1"), None)
    return jax.shard_map(on_device, mesh=torus, in_specs=(placed,) * 4, out_specs=(placed,) * 4, check_vma=False)
```
